512 devices in a mesh: dp: 64 (over z, x), seq: 8 (over y, core).
Axes of the slice: x: 4, y: 4, z: 16, core: 2. Of those that a mesh axis runs over, the one named last changes fastest.
Arguments:
- events: bfloat16 [64, 2048, 1024], P('dp', 'seq')
- w_project: bfloat16 [1024, 4096], P(None, 'seq'), may hold values from -0.1875 to 0.1875
- w_output: bfloat16 [1024, 1024], P('seq'), may hold values from -0.1875 to 0.1875
- rel_bias: float32 [8, 11], P('seq'), may hold values from -4 to 4
- in_gain: float32 [1024], replicated, may hold values from 0.5 to 1.5
- out_gain: float32 [1024], P('seq'), may hold values from 0.5 to 1.5
- user_ids: int32 [64, 2048], P('dp'), may hold values from 0 to 3, never falling along the last dimension, each value on 1 to 1024 neighbouring positions
- owner_dev: int32 [64, 2048], P('dp', 'seq'), may hold values from 0 to 63, as said below
- owner_row: int32 [64, 2048], P('dp', 'seq'), may hold values from 0 to 255, as said below
Outputs:
- layer_update: bfloat16 [64, 2048, 1024], P('dp', 'seq')
The draws below stay inside these ranges and needn't reach their ends.
Inputs may be any that keep to these rules, and one draw needn't show every extreme that they name: `owner_dev`: within each index of seq, a device sends to one index of dp either none of its rows or exactly 4 of them, and every device receives exactly 256 rows. `owner_row`: the owner rows that reach one device from all indices of dp are distinct and cover 0 to 255. `user_ids`: along the 2048 rows of each dp index the user number never falls; each user has 1 to 1024 rows and one has exactly 1024.
All inputs are finite; a program needn't handle non-finite values.
Results may differ from the reference program's by a relative error of at most 0.014.
Values may be sent and summed in bfloat16 or wider, within the bound.
A program may use at most 64 MiB of HBM per device.

```python
import math
import jax
import jax.numpy as jnp
import numpy as np
from jax import lax

D = 1024
HEADS = 8
HEAD = 128
BUCKETS = 11
USERS = 4
ROWS = 256
GROUP = 2048
CAP = 4
LONGEST = 1024
SPLITS = 8
LOCAL_HEADS = 1
N_DP = 64
N_SEQ = 8


def draw_events(key, part):
    first, second, third = jax.random.split(key, 3)
    row_scale = jnp.exp(jax.random.uniform(first, (N_DP, GROUP, 1), jnp.float32, math.log(0.3), math.log(3.0)))
    col_scale = jnp.exp(jax.random.uniform(second, (1, 1, D), jnp.float32, math.log(0.3), math.log(3.0)))
    values = jax.random.normal(third, (N_DP, GROUP, D), jnp.float32) * row_scale * col_scale
    return values.astype(jnp.bfloat16)


def route_tables(key):
    base = jax.random.fold_in(key, 17)
    groups = ROWS // CAP

    def column(column_key):
        keys = jax.random.split(column_key, 5)
        offsets = jax.random.permutation(keys[0], N_DP)[:groups].astype(jnp.int32)
        sigma = jax.random.permutation(keys[1], N_DP).astype(jnp.int32)
        tau = jax.random.permutation(keys[2], N_DP).astype(jnp.int32)
        sigma_inv = jnp.argsort(sigma).astype(jnp.int32)
        tau_inv = jnp.argsort(tau).astype(jnp.int32)
        row_perm = jax.vmap(lambda one_key: jax.random.permutation(one_key, ROWS).astype(jnp.int32))(jax.random.split(keys[3], N_DP))
        slot_perm = jax.vmap(lambda one_key: jax.random.permutation(one_key, ROWS).astype(jnp.int32))(jax.random.split(keys[4], N_DP))
        source = jnp.arange(N_DP, dtype=jnp.int32)[:, None]
        item = jnp.arange(ROWS, dtype=jnp.int32)[None, :]
        owner = tau_inv[(sigma_inv[source] - offsets[item // CAP]) % N_DP]
        place = row_perm[owner, item]
        owner_arr = jnp.zeros((N_DP, ROWS), jnp.int32).at[source, slot_perm].set(owner)
        place_arr = jnp.zeros((N_DP, ROWS), jnp.int32).at[source, slot_perm].set(place)
        return (owner_arr, place_arr)
    owners, places = jax.vmap(column)(jax.random.split(base, N_SEQ))
    owners = owners.transpose(1, 0, 2).reshape(N_DP, GROUP)
    places = places.transpose(1, 0, 2).reshape(N_DP, GROUP)
    return (owners, places)


def draw_owner_dev(key, part):
    return route_tables(key)[0]


def draw_owner_row(key, part):
    return route_tables(key)[1]


def steps_of(key, dims, cuts, smallest, largest):
    level, own = 1.0, jax.random.fold_in(key, 6)
    for dim, blocks in cuts:
        steps = jnp.exp(jax.random.uniform(jax.random.fold_in(own, dim), (blocks,), jnp.float32, smallest / len(cuts), largest / len(cuts)))
        level = level * jnp.repeat(steps, dims[dim] // blocks).reshape([-1 if axis == dim else 1 for axis in range(len(dims))])
    return level


def split_up(amount, total, most, lean):
    weights = [(1 << 20) // math.isqrt(rank ** lean) + 1 for rank in range(2, amount + 1)]
    rest, given = total - most - (amount - 1), [1] * (amount - 1)
    while rest > 0:
        movable = [i for i in range(amount - 1) if given[i] < most]
        mass, remaining = sum([weights[i] for i in movable]), rest
        for i in movable:
            extra = min(most - given[i], max(1, remaining * weights[i] // mass), rest)
            given[i] = given[i] + extra
            rest = rest - extra
    return np.array([most] + given)


def uneven(own_key, count, total, most, lean):
    if count == 2:
        one = jax.random.randint(own_key, (), max(1, total - most), min(most, total - 1) + 1)
        return jnp.stack([one, total - one])
    lengths = jnp.asarray(split_up(count, total, most, lean), jnp.int32)
    pairs = (count - 1) // 2
    source_of, receiver = lengths[1:1 + 2 * pairs:2], lengths[2:2 + 2 * pairs:2]
    slack = jnp.minimum(source_of - 1, most - receiver)
    shifted = jax.random.randint(jax.random.fold_in(own_key, 1), (pairs,), 0, 1 << 20) % (slack + 1)
    lengths = lengths.at[1:1 + 2 * pairs:2].set(source_of - shifted).at[2:2 + 2 * pairs:2].set(receiver + shifted)
    return lengths[jax.random.permutation(jax.random.fold_in(own_key, 2), count)]


def normal_values(own_key, extent, scale, reach, shards=(), kind=jnp.bfloat16):
    entries = scale * jax.random.normal(own_key, extent, jnp.float32)
    if shards:
        entries = entries * steps_of(own_key, extent, shards, -0.22, 0.18)
    return jnp.clip(entries, -reach, reach).astype(kind)


def setup_inputs(seed: int = 0) -> dict:
    seeds = jax.random.split(jax.random.key(seed), 10)
    events = draw_events(jax.random.fold_in(seeds[9], 71), 0)
    w_project = normal_values(seeds[1], (D, 4 * D), D ** -0.5, 0.1875, ((1, 8),))
    w_output = normal_values(seeds[2], (D, D), D ** -0.5, 0.1875, ((0, 8),))
    rel_bias = normal_values(seeds[3], (HEADS, BUCKETS), 1.0, 4.0, ((0, 8),), jnp.float32)
    in_gain = jnp.clip(1.0 + 0.1 * jax.random.normal(seeds[4], (D,), jnp.float32), 0.5, 1.5)
    out_gain = jnp.clip(1.0 + 0.1 * jax.random.normal(seeds[5], (D,), jnp.float32), 0.5, 1.5)
    user_ids = jax.vmap(lambda own: jnp.searchsorted(jnp.cumsum(uneven(own, USERS, GROUP, LONGEST, 2)), jnp.arange(GROUP), side="right"))(jax.random.split(seeds[6], N_DP)).reshape((N_DP, GROUP)).astype(jnp.int32)
    owner_dev = draw_owner_dev(jax.random.fold_in(seeds[9], 71), 0)
    owner_row = draw_owner_row(jax.random.fold_in(seeds[9], 71), 0)
    return dict(events=events, w_project=w_project, w_output=w_output, rel_bias=rel_bias, in_gain=in_gain, out_gain=out_gain, user_ids=user_ids, owner_dev=owner_dev, owner_row=owner_row)


EPSILON = 1e-05

def norm_rows(values, gain):
    average = lax.optimization_barrier(jnp.mean(values, axis=-1, keepdims=True))
    centred = values - average
    spread = lax.optimization_barrier(jnp.mean(centred * centred, axis=-1, keepdims=True))
    return centred * lax.rsqrt(spread + EPSILON) * gain

def bucket_bias(table, distance):
    total = jnp.zeros(distance.shape, jnp.float32) + table[0]
    for level in range(BUCKETS - 1):
        threshold = LONGEST // 2 ** (BUCKETS - 1 - level)
        total = total + jnp.where(distance >= threshold, table[level + 1] - table[level], jnp.zeros((), jnp.float32))
    return total

def reference(events, w_project, w_output, rel_bias, in_gain, out_gain, user_ids, owner_dev, owner_row):
    arrival = (jnp.arange(GROUP, dtype=jnp.int32) // ROWS * ROWS)[None, :]
    target = (owner_dev * GROUP + arrival + owner_row).reshape(-1).astype(jnp.int32)
    owned = jnp.zeros((N_DP * GROUP, D), jnp.bfloat16).at[target].set(events.reshape(-1, D)).reshape(N_DP, GROUP, D)
    position = jnp.arange(GROUP, dtype=jnp.int32)
    distance = position[:, None] - position[None, :]

    def group_layer(inputs):
        rows_in, segment = inputs
        normed = norm_rows(rows_in.astype(jnp.float32), in_gain).astype(jnp.bfloat16)
        projected = jax.nn.silu(jnp.dot(normed, w_project, preferred_element_type=jnp.float32)).astype(jnp.bfloat16)
        projected = projected.reshape(GROUP, HEADS, 4, HEAD)
        alive = (distance >= 0) & (segment[:, None] == segment[None, :])

        def one_head(head_idx):
            picked = lax.dynamic_index_in_dim(projected, head_idx, 1, keepdims=False)
            queries = picked[:, 0]
            key_rows = picked[:, 1]
            values = picked[:, 2]
            gate_rows = picked[:, 3]
            table = lax.dynamic_index_in_dim(rel_bias, head_idx, 0, keepdims=False)
            scores = jnp.dot(queries, key_rows.T, preferred_element_type=jnp.float32) * HEAD ** (-0.5) + bucket_bias(table, distance)
            weights = jnp.where(alive, jax.nn.silu(scores), jnp.zeros((), jnp.float32)).astype(jnp.bfloat16)
            mixed = jnp.dot(weights, values, preferred_element_type=jnp.float32)
            gain_part = lax.dynamic_slice_in_dim(out_gain, head_idx * HEAD, HEAD)
            return (norm_rows(mixed, gain_part) * gate_rows.astype(jnp.float32)).astype(jnp.bfloat16)
        gated = lax.map(one_head, jnp.arange(HEADS, dtype=jnp.int32))
        grouped = gated.reshape(SPLITS, LOCAL_HEADS, GROUP, HEAD).transpose(0, 2, 1, 3).reshape(SPLITS, GROUP, LOCAL_HEADS * HEAD)
        weights_out = w_output.reshape(SPLITS, LOCAL_HEADS * HEAD, D)
        partial_value = jnp.einsum('cgk,ckd->cgd', grouped.astype(jnp.float32), weights_out.astype(jnp.float32))
        partial_value = lax.optimization_barrier(partial_value.astype(jnp.bfloat16)).astype(jnp.float32)
        return lax.optimization_barrier(jnp.sum(partial_value, axis=0)).astype(jnp.bfloat16)
    merged = lax.map(group_layer, (owned, user_ids))
    return merged.reshape(-1, D)[target].reshape(N_DP, GROUP, D)
```

```python
import jax
import jax.numpy as jnp
from jax import lax
from jax.experimental import pallas as pl
from jax.experimental.pallas import tpu as pltpu
from jax.sharding import PartitionSpec as P

EPSILON = 1e-05
BLOCK = 256
FAR = -1e30


def norm_rows(values, gain):
    average = jnp.mean(values, axis=-1, keepdims=True)
    centred = values - average
    spread = jnp.mean(centred * centred, axis=-1, keepdims=True)
    return centred * lax.rsqrt(spread + EPSILON) * gain


def half_silu(half):
    return half + half * jnp.tanh(half)


def half_bias(table, offset, longest, levels):
    rows = lax.broadcasted_iota(jnp.int32, (BLOCK, BLOCK), 0)
    columns = lax.broadcasted_iota(jnp.int32, (BLOCK, BLOCK), 1)
    distance = rows - columns + offset * BLOCK
    total = jnp.full((BLOCK, BLOCK), table[0, 0], jnp.float32)
    for level in range(levels - 1):
        threshold = longest // 2 ** (levels - 1 - level)
        step = table[0, level + 1] - table[0, level]
        if threshold > offset * BLOCK + BLOCK - 1:
            continue
        if threshold <= offset * BLOCK - BLOCK + 1:
            total = total + step
        else:
            total = total + jnp.where(distance >= threshold, step, 0.0)
    total = 0.5 * total
    if offset == 0:
        total = jnp.where(distance >= 0, total, FAR)
    return total


def head_kernel(longest, table, x_ref, w_ref, gain_ref, row_ids, col_ids, out_ref, proj, bias, acc):
    step = pl.program_id(0)
    reach = bias.shape[0]
    width = acc.shape[1]

    @pl.when(step == 0)
    def _():
        for offset in range(reach):
            bias[offset] = half_bias(table, offset, longest, table.shape[1])

    here = pl.ds(pl.multiple_of(step * BLOCK, BLOCK), BLOCK)
    proj[here, :] = half_silu(
        0.5 * jnp.dot(x_ref[...], w_ref[...], preferred_element_type=jnp.float32)
    ).astype(jnp.bfloat16)
    ids = jnp.concatenate([col_ids[...]] * (BLOCK // col_ids.shape[1]), axis=1)
    scale = 0.5 * width ** (-0.5)

    def term(offset):
        first = pl.multiple_of((step - offset) * BLOCK, BLOCK)
        there = pl.ds(first, BLOCK)
        scores = lax.dot_general(
            proj[here, :width],
            proj[there, width : 2 * width],
            (((1,), (1,)), ((), ())),
            preferred_element_type=jnp.float32,
        )
        weights = half_silu(scores * scale + bias[offset])
        weights = jnp.where(ids == row_ids[:, there], weights, 0.0).astype(jnp.bfloat16)
        return jnp.dot(
            weights, proj[there, 2 * width : 3 * width], preferred_element_type=jnp.float32
        )

    acc[...] = term(0)
    for offset in range(1, reach):

        @pl.when(step >= offset)
        def _(offset=offset):
            acc[...] += term(offset)

    gate = proj[here, 3 * width :].astype(jnp.float32)
    out_ref[...] = (norm_rows(acc[...], gain_ref[...]) * gate).astype(jnp.bfloat16)


def heads(rows, w_project, table, gain, segment, longest):
    count, depth = rows.shape
    width = gain.shape[0]
    reach = longest // BLOCK + 1
    return pl.pallas_call(
        lambda *refs: head_kernel(longest, *refs),
        grid=(count // BLOCK,),
        out_shape=jax.ShapeDtypeStruct((count, width), jnp.bfloat16),
        in_specs=[
            pl.BlockSpec(memory_space=pltpu.SMEM),
            pl.BlockSpec((BLOCK, depth), lambda i: (i, 0)),
            pl.BlockSpec((depth, 4 * width), lambda i: (0, 0)),
            pl.BlockSpec((1, width), lambda i: (0, 0)),
            pl.BlockSpec((1, count), lambda i: (0, 0)),
            pl.BlockSpec((BLOCK, 128), lambda i: (i, 0)),
        ],
        out_specs=pl.BlockSpec((BLOCK, width), lambda i: (i, 0)),
        scratch_shapes=[
            pltpu.VMEM((count, 4 * width), jnp.bfloat16),
            pltpu.VMEM((reach, BLOCK, BLOCK), jnp.float32),
            pltpu.VMEM((BLOCK, width), jnp.float32),
        ],
        compiler_params=pltpu.CompilerParams(vmem_limit_bytes=32 << 20),
    )(
        table,
        rows,
        w_project,
        gain[None],
        segment,
        jnp.broadcast_to(segment.reshape(count, 1), (count, 128)),
    )


def pick(chosen, rows, dim):
    return lax.dot_general(
        chosen, rows, (((dim,), (0,)), ((), ())), preferred_element_type=jnp.float32
    ).astype(jnp.bfloat16)


def local(events, w_project, w_output, rel_bias, in_gain, out_gain, user_ids, owner_dev, owner_row):
    peers = lax.axis_size("dp")
    parts = lax.axis_size("seq")
    count, depth = events.shape[1:]
    each = count // peers
    owners = owner_dev[0]
    index = jnp.arange(count, dtype=jnp.int32)
    earlier = (owners[:, None] == owners[None, :]) & (index[None, :] < index[:, None])
    slot = owners * each + jnp.sum(earlier.astype(jnp.int32), axis=1)
    to_slot = (slot[None, :] == index[:, None]).astype(jnp.bfloat16)
    tagged = jnp.concatenate(
        [events[0], jnp.broadcast_to(owner_row[0][:, None], (count, 128)).astype(jnp.bfloat16)], axis=1
    )
    sent = pick(to_slot, tagged, 1)
    w_full = lax.all_gather(w_output, "seq", axis=0, tiled=True)
    got = lax.all_to_all(
        sent.reshape(peers, each, depth + 128), "dp", split_axis=0, concat_axis=0, tiled=True
    ).reshape(count, depth + 128)
    place = got[:, depth].astype(jnp.int32)
    to_place = (place[:, None] == index[None, :]).astype(jnp.bfloat16)
    normed = norm_rows(got[:, :depth].astype(jnp.float32), in_gain).astype(jnp.bfloat16)
    normed = pick(to_place, normed, 0)
    rows = lax.all_gather(normed, "seq", axis=0, tiled=True)
    gated = heads(rows, w_project, rel_bias, out_gain, user_ids, count * parts // 2)
    mine = lax.all_to_all(
        gated.reshape(parts, count, -1), "seq", split_axis=0, concat_axis=0, tiled=True
    )
    merged = jnp.einsum(
        "hrd,hdo->ro",
        mine,
        w_full.reshape(parts, -1, depth),
        preferred_element_type=jnp.float32,
    ).astype(jnp.bfloat16)
    returned = pick(to_place, merged, 1)
    home = lax.all_to_all(
        returned.reshape(peers, each, depth), "dp", split_axis=0, concat_axis=0, tiled=True
    ).reshape(count, depth)
    return pick(to_slot, home, 0)[None]


def solution(mesh):
    return jax.shard_map(
        local,
        mesh=mesh,
        in_specs=(
            P("dp", "seq", None),
            P(None, "seq"),
            P("seq", None),
            P("seq", None),
            P(),
            P("seq"),
            P("dp", None),
            P("dp", "seq"),
            P("dp", "seq"),
        ),
        out_specs=P("dp", "seq", None),
        check_vma=False,
    )
```

```python
import functools

import jax
import jax.numpy as jnp
from jax import lax
from jax.experimental import pallas as pl
from jax.experimental.pallas import tpu as pltpu
from jax.sharding import PartitionSpec as P

EPSILON = 1e-05
BLOCK = 256
FAR = -1e30
MESH = pl.DeviceIdType.MESH


def norm_rows(values, gain):
    average = jnp.mean(values, axis=-1, keepdims=True)
    centred = values - average
    spread = jnp.mean(centred * centred, axis=-1, keepdims=True)
    return centred * lax.rsqrt(spread + EPSILON) * gain


def half_silu(half):
    return half + half * jnp.tanh(half)


def half_bias(table, offset, longest, levels):
    rows = lax.broadcasted_iota(jnp.int32, (BLOCK, BLOCK), 0)
    columns = lax.broadcasted_iota(jnp.int32, (BLOCK, BLOCK), 1)
    distance = rows - columns + offset * BLOCK
    total = jnp.full((BLOCK, BLOCK), table[0, 0], jnp.float32)
    for level in range(levels - 1):
        threshold = longest // 2 ** (levels - 1 - level)
        step = table[0, level + 1] - table[0, level]
        if threshold > offset * BLOCK + BLOCK - 1:
            continue
        if threshold <= offset * BLOCK - BLOCK + 1:
            total = total + step
        else:
            total = total + jnp.where(distance >= threshold, step, 0.0)
    total = 0.5 * total
    if offset == 0:
        total = jnp.where(distance >= 0, total, FAR)
    return total


def head_kernel(longest, table, x_ref, w_ref, gain_ref, row_ids, col_ids, out_ref, proj, bias, acc):
    step = pl.program_id(0)
    reach = bias.shape[0]
    width = acc.shape[1]

    @pl.when(step == 0)
    def _():
        for offset in range(reach):
            bias[offset] = half_bias(table, offset, longest, table.shape[1])

    here = pl.ds(pl.multiple_of(step * BLOCK, BLOCK), BLOCK)
    proj[here, :] = half_silu(
        0.5 * jnp.dot(x_ref[...], w_ref[...], preferred_element_type=jnp.float32)
    ).astype(jnp.bfloat16)
    ids = jnp.concatenate([col_ids[...]] * (BLOCK // col_ids.shape[1]), axis=1)
    scale = 0.5 * width ** (-0.5)

    def term(offset):
        first = pl.multiple_of((step - offset) * BLOCK, BLOCK)
        there = pl.ds(first, BLOCK)
        scores = lax.dot_general(
            proj[here, :width],
            proj[there, width : 2 * width],
            (((1,), (1,)), ((), ())),
            preferred_element_type=jnp.float32,
        )
        weights = half_silu(scores * scale + bias[offset])
        weights = jnp.where(ids == row_ids[:, there], weights, 0.0).astype(jnp.bfloat16)
        return jnp.dot(
            weights, proj[there, 2 * width : 3 * width], preferred_element_type=jnp.float32
        )

    acc[...] = term(0)
    for offset in range(1, reach):

        @pl.when(step >= offset)
        def _(offset=offset):
            acc[...] += term(offset)

    gate = proj[here, 3 * width :].astype(jnp.float32)
    out_ref[...] = (norm_rows(acc[...], gain_ref[...]) * gate).astype(jnp.bfloat16)


def heads(rows, w_project, table, gain, segment, longest):
    count, depth = rows.shape
    width = gain.shape[0]
    reach = longest // BLOCK + 1
    return pl.pallas_call(
        lambda *refs: head_kernel(longest, *refs),
        grid=(count // BLOCK,),
        out_shape=jax.ShapeDtypeStruct((count, width), jnp.bfloat16),
        in_specs=[
            pl.BlockSpec(memory_space=pltpu.SMEM),
            pl.BlockSpec((BLOCK, depth), lambda i: (i, 0)),
            pl.BlockSpec((depth, 4 * width), lambda i: (0, 0)),
            pl.BlockSpec((1, width), lambda i: (0, 0)),
            pl.BlockSpec((1, count), lambda i: (0, 0)),
            pl.BlockSpec((BLOCK, 128), lambda i: (i, 0)),
        ],
        out_specs=pl.BlockSpec((BLOCK, width), lambda i: (i, 0)),
        scratch_shapes=[
            pltpu.VMEM((count, 4 * width), jnp.bfloat16),
            pltpu.VMEM((reach, BLOCK, BLOCK), jnp.float32),
            pltpu.VMEM((BLOCK, width), jnp.float32),
        ],
        compiler_params=pltpu.CompilerParams(vmem_limit_bytes=32 << 20),
    )(
        table,
        rows,
        w_project,
        gain[None],
        segment,
        jnp.broadcast_to(segment.reshape(count, 1), (count, 128)),
    )


def reach_all(barrier, places):
    for place in places:
        pl.semaphore_signal(barrier, inc=1, device_id=place, device_id_type=MESH)


def dp_exchange(count, start_copy):
    start_copy(count // 2)

    @pl.loop(1, count // 2)
    def _(step):
        start_copy(count // 2 - step)
        start_copy(count // 2 + step)


def enter_kernel(count, sent, shard, got, full, out_sem, in_sem, own_sem, w_out, w_in):
    me = lax.axis_index("dp")
    seat = lax.axis_index("seq")
    seats = lax.axis_size("seq")
    partner = seat + 1 - 2 * (seat % 2)
    barrier = pltpu.get_barrier_semaphore()

    @pl.loop(1, count)
    def _(distance):
        pl.semaphore_signal(
            barrier, inc=1, device_id={"dp": (me + distance) % count}, device_id_type=MESH
        )

    reach_all(barrier, [{"seq": partner}] + [{"seq": (seat + 2 * k) % seats} for k in (1, 2, 3)])
    pl.semaphore_wait(barrier, count - 1 + 4)

    def row_copy(distance):
        peer = (me + distance) % count
        return pltpu.make_async_remote_copy(
            src_ref=sent.at[peer],
            dst_ref=got.at[me],
            send_sem=out_sem.at[distance],
            recv_sem=in_sem.at[distance],
            device_id={"dp": peer},
            device_id_type=MESH,
        )

    dp_exchange(count, lambda distance: row_copy(distance).start())
    own = pltpu.make_async_copy(sent.at[me], got.at[me], own_sem.at[0])
    own.start()
    own_w = pltpu.make_async_copy(shard, full.at[seat], own_sem.at[1])
    own_w.start()

    def to_chip(k):
        return pltpu.make_async_remote_copy(
            src_ref=shard,
            dst_ref=full.at[seat],
            send_sem=w_out.at[k],
            recv_sem=w_in.at[k],
            device_id={"seq": (seat + 2 * k) % seats},
            device_id_type=MESH,
        )

    def to_partner(k):
        block = full.at[(seat + seats - 2 * k) % seats]
        return pltpu.make_async_remote_copy(
            src_ref=shard if k == 0 else block,
            dst_ref=block,
            send_sem=w_out.at[4 + k],
            recv_sem=w_in.at[4 + k],
            device_id={"seq": partner},
            device_id_type=MESH,
        )

    for k in (1, 2, 3):
        to_chip(k).start()
    to_partner(0).start()
    for k in (1, 3, 2):
        to_chip(k).wait_recv()
        to_partner(k).start()
    for k in (1, 2, 3):
        to_chip(k).wait_send()
    for k in range(4):
        to_partner(k).wait()

    @pl.loop(1, count)
    def _(distance):
        row_copy(distance).wait()

    own.wait()
    own_w.wait()


def gather_kernel(block_in, full, ring_out, ring_in, pair_out, pair_in, own_sem):
    seat = lax.axis_index("seq")
    seats = lax.axis_size("seq")
    partner = seat + 1 - 2 * (seat % 2)
    right, left = (seat + 2) % seats, (seat + seats - 2) % seats
    across = (seat + 4) % seats
    half = block_in.shape[0] // 2
    barrier = pltpu.get_barrier_semaphore()
    reach_all(barrier, [{"seq": partner}, {"seq": right}, {"seq": left}])
    pl.semaphore_wait(barrier, 3)

    def piece(ref, part):
        return ref.at[pl.ds(part * half, half)]

    def ring(slot, source, owner, part, target):
        return pltpu.make_async_remote_copy(
            src_ref=piece(source, part),
            dst_ref=piece(full.at[owner], part),
            send_sem=ring_out.at[slot],
            recv_sem=ring_in.at[slot],
            device_id={"seq": target},
            device_id_type=MESH,
        )

    def pair(slot, source, owner, part):
        return pltpu.make_async_remote_copy(
            src_ref=piece(source, part),
            dst_ref=piece(full.at[owner], part),
            send_sem=pair_out.at[slot],
            recv_sem=pair_in.at[slot],
            device_id={"seq": partner},
            device_id_type=MESH,
        )

    firsts = [
        ring(0, block_in, seat, 0, right),
        ring(1, block_in, seat, 1, left),
        ring(2, block_in, seat, 1, right),
        ring(3, block_in, seat, 0, left),
    ]
    for copy in firsts:
        copy.start()
    own = pltpu.make_async_copy(block_in, full.at[seat], own_sem)
    own.start()
    pairs = [pair(0, block_in, seat, 0), pair(1, block_in, seat, 1)]
    pairs[0].start()
    pairs[1].start()
    seconds = [
        ring(4, full.at[left], left, 0, right),
        ring(5, full.at[right], right, 1, left),
    ]
    arrivals = [(left, 0), (right, 1), (left, 1), (right, 0), (across, 0), (across, 1)]
    for slot, (owner, part) in enumerate(arrivals):
        (firsts[slot] if slot < 4 else seconds[slot - 4]).wait_recv()
        if slot < 2:
            seconds[slot].start()
        pairs.append(pair(2 + slot, full.at[owner], owner, part))
        pairs[-1].start()
    for copy in firsts + seconds:
        copy.wait_send()
    for copy in pairs:
        copy.wait()
    own.wait()


def swap_kernel(axis, count, sent, got, out_sem, in_sem, own_sem):
    me = lax.axis_index(axis)
    barrier = pltpu.get_barrier_semaphore()

    @pl.loop(1, count)
    def _(distance):
        pl.semaphore_signal(
            barrier, inc=1, device_id={axis: (me + distance) % count}, device_id_type=MESH
        )

    pl.semaphore_wait(barrier, count - 1)

    def copy(distance):
        peer = (me + distance) % count
        return pltpu.make_async_remote_copy(
            src_ref=sent.at[peer],
            dst_ref=got.at[me],
            send_sem=out_sem.at[distance],
            recv_sem=in_sem.at[distance],
            device_id={axis: peer},
            device_id_type=MESH,
        )

    dp_exchange(count, lambda distance: copy(distance).start())
    own = pltpu.make_async_copy(sent.at[me], got.at[me], own_sem)
    own.start()

    @pl.loop(1, count)
    def _(distance):
        copy(distance).wait()

    own.wait()


IN_VMEM = pl.BlockSpec(memory_space=pltpu.VMEM)
DMA = pltpu.SemaphoreType.DMA


def remote(kernel, number, operands, shapes, scratch):
    return pl.pallas_call(
        kernel,
        out_shape=tuple(jax.ShapeDtypeStruct(shape, jnp.bfloat16) for shape in shapes),
        in_specs=[IN_VMEM] * len(operands),
        out_specs=(IN_VMEM,) * len(shapes),
        scratch_shapes=scratch,
        compiler_params=pltpu.CompilerParams(
            collective_id=number, has_side_effects=True, vmem_limit_bytes=32 << 20
        ),
    )(*operands)


def enter(sent, shard):
    count, seats = lax.axis_size("dp"), lax.axis_size("seq")
    return remote(
        functools.partial(enter_kernel, count),
        0,
        (sent, shard),
        (sent.shape, (seats,) + shard.shape),
        [DMA((count,)), DMA((count,)), DMA((2,)), DMA((8,)), DMA((8,))],
    )


def gather(block):
    seats = lax.axis_size("seq")
    return remote(
        gather_kernel,
        1,
        (block,),
        ((seats,) + block.shape,),
        [DMA((6,)), DMA((6,)), DMA((8,)), DMA((8,)), DMA(())],
    )[0]


def swap(sent, axis, number):
    count = lax.axis_size(axis)
    return remote(
        functools.partial(swap_kernel, axis, count),
        number,
        (sent,),
        (sent.shape,),
        [DMA((count,)), DMA((count,)), DMA(())],
    )[0]


def pick(chosen, rows, dim):
    return lax.dot_general(
        chosen, rows, (((dim,), (0,)), ((), ())), preferred_element_type=jnp.float32
    ).astype(jnp.bfloat16)


def local(events, w_project, w_output, rel_bias, in_gain, out_gain, user_ids, owner_dev, owner_row):
    peers = lax.axis_size("dp")
    parts = lax.axis_size("seq")
    count, depth = events.shape[1:]
    each = count // peers
    owners = owner_dev[0]
    index = jnp.arange(count, dtype=jnp.int32)
    earlier = (owners[:, None] == owners[None, :]) & (index[None, :] < index[:, None])
    slot = owners * each + jnp.sum(earlier.astype(jnp.int32), axis=1)
    to_slot = (slot[None, :] == index[:, None]).astype(jnp.bfloat16)
    tagged = jnp.concatenate(
        [events[0], jnp.broadcast_to(owner_row[0][:, None], (count, 128)).astype(jnp.bfloat16)], axis=1
    )
    sent = pick(to_slot, tagged, 1)
    got, w_full = enter(sent.reshape(peers, each, depth + 128), w_output)
    got = got.reshape(count, depth + 128)
    place = got[:, depth].astype(jnp.int32)
    to_place = (place[:, None] == index[None, :]).astype(jnp.bfloat16)
    normed = norm_rows(got[:, :depth].astype(jnp.float32), in_gain).astype(jnp.bfloat16)
    normed = pick(to_place, normed, 0)
    rows = gather(normed).reshape(parts * count, depth)
    gated = heads(rows, w_project, rel_bias, out_gain, user_ids, count * parts // 2)
    mine = swap(gated.reshape(parts, count, -1), "seq", 2)
    merged = jnp.einsum(
        "hrd,hdo->ro",
        mine,
        w_full,
        preferred_element_type=jnp.float32,
    ).astype(jnp.bfloat16)
    returned = pick(to_place, merged, 1)
    home = swap(returned.reshape(peers, each, depth), "dp", 3).reshape(count, depth)
    return pick(to_slot, home, 0)[None]


def solution(mesh):
    return jax.shard_map(
        local,
        mesh=mesh,
        in_specs=(
            P("dp", "seq", None),
            P(None, "seq"),
            P("seq", None),
            P("seq", None),
            P(),
            P("seq"),
            P("dp", None),
            P("dp", "seq"),
            P("dp", "seq"),
        ),
        out_specs=P("dp", "seq", None),
        check_vma=False,
    )
```

```python
import functools

import jax
import jax.numpy as jnp
from jax import lax
from jax.experimental import pallas as pl
from jax.experimental.pallas import tpu as pltpu
from jax.sharding import PartitionSpec as P

EPSILON = 1e-05
BLOCK = 256
FAR = -1e30
MESH = pl.DeviceIdType.MESH


def norm_rows(values, gain):
    average = jnp.mean(values, axis=-1, keepdims=True)
    centred = values - average
    spread = jnp.mean(centred * centred, axis=-1, keepdims=True)
    return centred * lax.rsqrt(spread + EPSILON) * gain


def half_silu(half):
    return half + half * jnp.tanh(half)


def half_bias(table, offset, longest, levels):
    rows = lax.broadcasted_iota(jnp.int32, (BLOCK, BLOCK), 0)
    columns = lax.broadcasted_iota(jnp.int32, (BLOCK, BLOCK), 1)
    distance = rows - columns + offset * BLOCK
    total = jnp.full((BLOCK, BLOCK), table[0, 0], jnp.float32)
    for level in range(levels - 1):
        threshold = longest // 2 ** (levels - 1 - level)
        step = table[0, level + 1] - table[0, level]
        if threshold > offset * BLOCK + BLOCK - 1:
            continue
        if threshold <= offset * BLOCK - BLOCK + 1:
            total = total + step
        else:
            total = total + jnp.where(distance >= threshold, step, 0.0)
    total = 0.5 * total
    if offset == 0:
        total = jnp.where(distance >= 0, total, FAR)
    return total


def reach_all(barrier, places):
    for place in places:
        pl.semaphore_signal(barrier, inc=1, device_id=place, device_id_type=MESH)


def dp_exchange(count, start_copy):
    start_copy(count // 2)

    @pl.loop(1, count // 2)
    def _(step):
        start_copy(count // 2 - step)
        start_copy(count // 2 + step)


def enter_kernel(count, sent, shard, got, full, out_sem, in_sem, own_sem, w_out, w_in):
    me = lax.axis_index("dp")
    seat = lax.axis_index("seq")
    seats = lax.axis_size("seq")
    partner = seat + 1 - 2 * (seat % 2)
    barrier = pltpu.get_barrier_semaphore()

    @pl.loop(1, count)
    def _(distance):
        pl.semaphore_signal(
            barrier, inc=1, device_id={"dp": (me + distance) % count}, device_id_type=MESH
        )

    reach_all(barrier, [{"seq": partner}] + [{"seq": (seat + 2 * k) % seats} for k in (1, 2, 3)])
    pl.semaphore_wait(barrier, count - 1 + 4)

    def row_copy(distance):
        peer = (me + distance) % count
        return pltpu.make_async_remote_copy(
            src_ref=sent.at[peer],
            dst_ref=got.at[me],
            send_sem=out_sem.at[distance],
            recv_sem=in_sem.at[distance],
            device_id={"dp": peer},
            device_id_type=MESH,
        )

    dp_exchange(count, lambda distance: row_copy(distance).start())
    own = pltpu.make_async_copy(sent.at[me], got.at[me], own_sem.at[0])
    own.start()
    own_w = pltpu.make_async_copy(shard, full.at[seat], own_sem.at[1])
    own_w.start()

    def to_chip(k):
        return pltpu.make_async_remote_copy(
            src_ref=shard,
            dst_ref=full.at[seat],
            send_sem=w_out.at[k],
            recv_sem=w_in.at[k],
            device_id={"seq": (seat + 2 * k) % seats},
            device_id_type=MESH,
        )

    def to_partner(k):
        block = full.at[(seat + seats - 2 * k) % seats]
        return pltpu.make_async_remote_copy(
            src_ref=shard if k == 0 else block,
            dst_ref=block,
            send_sem=w_out.at[4 + k],
            recv_sem=w_in.at[4 + k],
            device_id={"seq": partner},
            device_id_type=MESH,
        )

    for k in (1, 2, 3):
        to_chip(k).start()
    to_partner(0).start()
    for k in (1, 3, 2):
        to_chip(k).wait_recv()
        to_partner(k).start()
    for k in (1, 2, 3):
        to_chip(k).wait_send()
    for k in range(4):
        to_partner(k).wait()

    @pl.loop(1, count)
    def _(distance):
        row_copy(distance).wait()

    own.wait()
    own_w.wait()


def gather_kernel(block_in, w_ref, proj, full, ring_out, ring_in, pair_out, pair_in):
    seat = lax.axis_index("seq")
    seats = lax.axis_size("seq")
    partner = seat + 1 - 2 * (seat % 2)
    right, left = (seat + 2) % seats, (seat + seats - 2) % seats
    across = (seat + 4) % seats
    rows = block_in.shape[0]
    half = rows // 2
    barrier = pltpu.get_barrier_semaphore()
    reach_all(barrier, [{"seq": partner}, {"seq": right}, {"seq": left}])
    pl.semaphore_wait(barrier, 3)

    def piece(ref, part):
        return ref.at[pl.ds(part * half, half)]

    def ring(slot, source, owner, part, target):
        return pltpu.make_async_remote_copy(
            src_ref=piece(source, part),
            dst_ref=piece(full.at[owner], part),
            send_sem=ring_out.at[slot],
            recv_sem=ring_in.at[slot],
            device_id={"seq": target},
            device_id_type=MESH,
        )

    def pair(slot, source, owner, part):
        return pltpu.make_async_remote_copy(
            src_ref=piece(source, part),
            dst_ref=piece(full.at[owner], part),
            send_sem=pair_out.at[slot],
            recv_sem=pair_in.at[slot],
            device_id={"seq": partner},
            device_id_type=MESH,
        )

    firsts = [
        ring(0, block_in, seat, 0, right),
        ring(1, block_in, seat, 1, left),
        ring(2, block_in, seat, 1, right),
        ring(3, block_in, seat, 0, left),
    ]
    for copy in firsts:
        copy.start()
    pairs = [pair(0, block_in, seat, 0), pair(1, block_in, seat, 1)]
    pairs[0].start()
    pairs[1].start()
    seconds = [
        ring(4, full.at[left], left, 0, right),
        ring(5, full.at[right], right, 1, left),
    ]

    def project(block, owner):
        there = pl.ds(pl.multiple_of(owner * rows, rows), rows)
        proj[there, :] = half_silu(
            0.5 * jnp.dot(block[...], w_ref[...], preferred_element_type=jnp.float32)
        ).astype(jnp.bfloat16)

    project(block_in, seat)
    pairs[0].wait_recv()
    pairs[1].wait_recv()
    project(full.at[partner], partner)
    arrivals = [(left, 0), (right, 1), (left, 1), (right, 0), (across, 0), (across, 1)]
    for slot, (owner, part) in enumerate(arrivals):
        (firsts[slot] if slot < 4 else seconds[slot - 4]).wait_recv()
        if slot < 2:
            seconds[slot].start()
        pairs.append(pair(2 + slot, full.at[owner], owner, part))
        pairs[-1].start()
        if slot == 3:
            project(full.at[left], left)
            project(full.at[right], right)
            for early in (2, 3, 4, 5):
                pairs[early].wait_recv()
            for owner in (left, right):
                other = owner + 1 - 2 * (owner % 2)
                project(full.at[other], other)
    project(full.at[across], across)
    pairs[6].wait_recv()
    pairs[7].wait_recv()
    other = across + 1 - 2 * (across % 2)
    project(full.at[other], other)
    for copy in firsts + seconds + pairs:
        copy.wait_send()


def tail_kernel(
    longest, peers, table, proj, gain_ref, row_ids, col_ids, w_full, to_place, home,
    bias, acc, gated, mine, returned, swap_out, swap_in, back_out, back_in, own_sem,
):
    me = lax.axis_index("dp")
    seat = lax.axis_index("seq")
    seats = lax.axis_size("seq")
    reach = bias.shape[0]
    width = acc.shape[1]
    barrier = pltpu.get_barrier_semaphore()

    @pl.loop(1, peers)
    def _(distance):
        pl.semaphore_signal(
            barrier, inc=1, device_id={"dp": (me + distance) % peers}, device_id_type=MESH
        )

    reach_all(barrier, [{"seq": (seat + k) % seats} for k in range(1, seats)])

    for offset in range(reach):
        bias[offset] = half_bias(table, offset, longest, table.shape[1])
    scale = 0.5 * width ** (-0.5)

    def swap(distance):
        return pltpu.make_async_remote_copy(
            src_ref=gated.at[(seat + distance) % seats],
            dst_ref=mine.at[seat],
            send_sem=swap_out.at[distance],
            recv_sem=swap_in.at[distance],
            device_id={"seq": (seat + distance) % seats},
            device_id_type=MESH,
        )

    @pl.loop(1, seats + 1)
    def _(distance):
        block = (seat + distance) % seats
        here = pl.ds(pl.multiple_of(block * BLOCK, BLOCK), BLOCK)
        ids = jnp.concatenate([col_ids[here, :]] * (BLOCK // col_ids.shape[1]), axis=1)

        def term(offset):
            there = pl.ds(pl.multiple_of((block - offset) * BLOCK, BLOCK), BLOCK)
            scores = lax.dot_general(
                proj[here, :width],
                proj[there, width : 2 * width],
                (((1,), (1,)), ((), ())),
                preferred_element_type=jnp.float32,
            )
            weights = half_silu(scores * scale + bias[offset])
            weights = jnp.where(ids == row_ids[:, there], weights, 0.0).astype(jnp.bfloat16)
            return jnp.dot(
                weights, proj[there, 2 * width : 3 * width], preferred_element_type=jnp.float32
            )

        acc[...] = term(0)

        @pl.when(distance == 2)
        def _():
            pl.semaphore_wait(barrier, peers - 1 + seats - 1)

        @pl.when(distance >= 2)
        def _():
            swap(distance - 1).start()

        for offset in range(1, reach):

            @pl.when(block >= offset)
            def _(offset=offset):
                acc[...] += term(offset)

        gate = proj[here, 3 * width :].astype(jnp.float32)
        gated[block] = (norm_rows(acc[...], gain_ref[...]) * gate).astype(jnp.bfloat16)

    mine[seat] = gated[seat]
    for distance in range(1, seats):
        swap(distance).wait_recv()
    rows = jnp.concatenate([mine[head] for head in range(seats)], axis=1)
    merged = jnp.dot(rows, w_full[...], preferred_element_type=jnp.float32).astype(jnp.bfloat16)
    picked = jnp.dot(to_place[...], merged, preferred_element_type=jnp.float32)
    returned[...] = picked.reshape(returned.shape).astype(jnp.bfloat16)
    for distance in range(1, seats):
        swap(distance).wait_send()

    def back(distance):
        peer = (me + distance) % peers
        return pltpu.make_async_remote_copy(
            src_ref=returned.at[peer],
            dst_ref=home.at[me],
            send_sem=back_out.at[distance],
            recv_sem=back_in.at[distance],
            device_id={"dp": peer},
            device_id_type=MESH,
        )

    dp_exchange(peers, lambda distance: back(distance).start())
    own = pltpu.make_async_copy(returned.at[me], home.at[me], own_sem)
    own.start()

    @pl.loop(1, peers)
    def _(distance):
        back(distance).wait()

    own.wait()


IN_VMEM = pl.BlockSpec(memory_space=pltpu.VMEM)
DMA = pltpu.SemaphoreType.DMA


def remote(kernel, number, operands, shapes, scratch):
    return pl.pallas_call(
        kernel,
        out_shape=tuple(jax.ShapeDtypeStruct(shape, jnp.bfloat16) for shape in shapes),
        in_specs=[IN_VMEM] * len(operands),
        out_specs=(IN_VMEM,) * len(shapes),
        scratch_shapes=scratch,
        compiler_params=pltpu.CompilerParams(
            collective_id=number, has_side_effects=True, vmem_limit_bytes=32 << 20
        ),
    )(*operands)


def enter(sent, shard):
    count, seats = lax.axis_size("dp"), lax.axis_size("seq")
    return remote(
        functools.partial(enter_kernel, count),
        0,
        (sent, shard),
        (sent.shape, (seats,) + shard.shape),
        [DMA((count,)), DMA((count,)), DMA((2,)), DMA((8,)), DMA((8,))],
    )


def gather(block, w_project):
    seats = lax.axis_size("seq")
    rows, depth = block.shape
    return remote(
        gather_kernel,
        1,
        (block, w_project),
        ((seats * rows, w_project.shape[1]),),
        [pltpu.VMEM((seats, rows, depth), jnp.bfloat16), DMA((6,)), DMA((6,)), DMA((8,)), DMA((8,))],
    )[0]


def tail(proj, table, gain, segment, w_full, to_place):
    peers, seats = lax.axis_size("dp"), lax.axis_size("seq")
    count, (width,), depth = proj.shape[0], gain.shape, w_full.shape[1]
    rows = to_place.shape[0]
    reach = count // 2 // BLOCK + 1
    return pl.pallas_call(
        functools.partial(tail_kernel, count // 2, peers),
        out_shape=jax.ShapeDtypeStruct((peers, rows // peers, depth), jnp.bfloat16),
        in_specs=[pl.BlockSpec(memory_space=pltpu.SMEM)] + [IN_VMEM] * 6,
        out_specs=IN_VMEM,
        scratch_shapes=[
            pltpu.VMEM((reach, BLOCK, BLOCK), jnp.float32),
            pltpu.VMEM((BLOCK, width), jnp.float32),
            pltpu.VMEM((seats, rows, width), jnp.bfloat16),
            pltpu.VMEM((seats, rows, width), jnp.bfloat16),
            pltpu.VMEM((peers, rows // peers, depth), jnp.bfloat16),
            DMA((seats,)),
            DMA((seats,)),
            DMA((peers,)),
            DMA((peers,)),
            DMA(()),
        ],
        compiler_params=pltpu.CompilerParams(
            collective_id=2, has_side_effects=True, vmem_limit_bytes=32 << 20
        ),
    )(
        table,
        proj,
        gain[None],
        segment,
        jnp.broadcast_to(segment.reshape(count, 1), (count, 128)),
        w_full,
        to_place,
    )


def pick(chosen, rows, dim):
    return lax.dot_general(
        chosen, rows, (((dim,), (0,)), ((), ())), preferred_element_type=jnp.float32
    ).astype(jnp.bfloat16)


def local(events, w_project, w_output, rel_bias, in_gain, out_gain, user_ids, owner_dev, owner_row):
    peers = lax.axis_size("dp")
    count, depth = events.shape[1:]
    each = count // peers
    owners = owner_dev[0]
    index = jnp.arange(count, dtype=jnp.int32)
    earlier = (owners[:, None] == owners[None, :]) & (index[None, :] < index[:, None])
    slot = owners * each + jnp.sum(earlier.astype(jnp.int32), axis=1)
    to_slot = (slot[None, :] == index[:, None]).astype(jnp.bfloat16)
    tagged = jnp.concatenate(
        [events[0], jnp.broadcast_to(owner_row[0][:, None], (count, 128)).astype(jnp.bfloat16)], axis=1
    )
    sent = pick(to_slot, tagged, 1)
    got, w_full = enter(sent.reshape(peers, each, depth + 128), w_output)
    got = got.reshape(count, depth + 128)
    place = got[:, depth].astype(jnp.int32)
    to_place = (place[:, None] == index[None, :]).astype(jnp.bfloat16)
    normed = norm_rows(got[:, :depth].astype(jnp.float32), in_gain).astype(jnp.bfloat16)
    normed = pick(to_place, normed, 0)
    proj = gather(normed, w_project)
    home = tail(proj, rel_bias, out_gain, user_ids, w_full.reshape(-1, depth), to_place)
    home = home.reshape(count, depth)
    return pick(to_slot, home, 0)[None]


def solution(mesh):
    return jax.shard_map(
        local,
        mesh=mesh,
        in_specs=(
            P("dp", "seq", None),
            P(None, "seq"),
            P("seq", None),
            P("seq", None),
            P(),
            P("seq"),
            P("dp", None),
            P("dp", "seq"),
            P("dp", "seq"),
        ),
        out_specs=P("dp", "seq", None),
        check_vma=False,
    )
```

```python
import functools

import jax
import jax.numpy as jnp
from jax import lax
from jax.experimental import pallas as pl
from jax.experimental.pallas import tpu as pltpu
from jax.sharding import PartitionSpec as P

EPSILON = 1e-05
BLOCK = 256
FAR = -1e30
MESH = pl.DeviceIdType.MESH


def norm_rows(values, gain):
    average = jnp.mean(values, axis=-1, keepdims=True)
    centred = values - average
    spread = jnp.mean(centred * centred, axis=-1, keepdims=True)
    return centred * lax.rsqrt(spread + EPSILON) * gain


def half_silu(half):
    return half + half * jnp.tanh(half)


def half_bias(table, offset, longest, levels):
    rows = lax.broadcasted_iota(jnp.int32, (BLOCK, BLOCK), 0)
    columns = lax.broadcasted_iota(jnp.int32, (BLOCK, BLOCK), 1)
    distance = rows - columns + offset * BLOCK
    total = jnp.full((BLOCK, BLOCK), table[0, 0], jnp.float32)
    for level in range(levels - 1):
        threshold = longest // 2 ** (levels - 1 - level)
        step = table[0, level + 1] - table[0, level]
        if threshold > offset * BLOCK + BLOCK - 1:
            continue
        if threshold <= offset * BLOCK - BLOCK + 1:
            total = total + step
        else:
            total = total + jnp.where(distance >= threshold, step, 0.0)
    total = 0.5 * total
    if offset == 0:
        total = jnp.where(distance >= 0, total, FAR)
    return total


def reach_all(barrier, places):
    for place in places:
        pl.semaphore_signal(barrier, inc=1, device_id=place, device_id_type=MESH)


def far_first(turn, count):
    return count // 2 - (turn + 1) // 2 * (2 * (turn % 2) - 1)


def enter_kernel(
    count, quarters, sent, shard, gain, w_ref, full_w, proj, to_place,
    got, full, mixed, out_sem, in_sem, w_out, w_in, ring_out, ring_in, pair_out, pair_in, own_sem,
):
    me = lax.axis_index("dp")
    seat = lax.axis_index("seq")
    seats = lax.axis_size("seq")
    partner = seat + 1 - 2 * (seat % 2)
    right, left, across = (seat + 2) % seats, (seat + seats - 2) % seats, (seat + 4) % seats
    turns = count // quarters
    rows = full.shape[2]
    depth = gain.shape[1]
    barrier = pltpu.get_barrier_semaphore()

    @pl.loop(1, count)
    def _(distance):
        pl.semaphore_signal(
            barrier, inc=1, device_id={"dp": (me + distance) % count}, device_id_type=MESH
        )

    reach_all(barrier, [{"seq": place} for place in (partner, right, left, across)])
    pl.semaphore_wait(barrier, count - 1 + 4)

    def row_copy(turn):
        peer = (me + far_first(turn, count)) % count
        return pltpu.make_async_remote_copy(
            src_ref=sent.at[peer],
            dst_ref=got.at[turn],
            send_sem=out_sem.at[turn],
            recv_sem=in_sem.at[turn],
            device_id={"dp": peer},
            device_id_type=MESH,
        )

    @pl.loop(0, count - 1)
    def _(turn):
        row_copy(turn).start()

    own = pltpu.make_async_copy(sent.at[me], got.at[count - 1], own_sem.at[0])
    own.start()
    own_w = pltpu.make_async_copy(shard, full_w.at[seat], own_sem.at[1])
    own_w.start()

    def to_chip(k):
        return pltpu.make_async_remote_copy(
            src_ref=shard,
            dst_ref=full_w.at[seat],
            send_sem=w_out.at[k],
            recv_sem=w_in.at[k],
            device_id={"seq": (seat + 2 * k) % seats},
            device_id_type=MESH,
        )

    def to_partner(k):
        block = full_w.at[(seat + seats - 2 * k) % seats]
        return pltpu.make_async_remote_copy(
            src_ref=shard if k == 0 else block,
            dst_ref=block,
            send_sem=w_out.at[4 + k],
            recv_sem=w_in.at[4 + k],
            device_id={"seq": partner},
            device_id_type=MESH,
        )

    def send(quarter, owner, target, out_sems, in_sems, slot):
        block = full.at[quarter, owner]
        return pltpu.make_async_remote_copy(
            src_ref=block,
            dst_ref=block,
            send_sem=out_sems.at[quarter, slot],
            recv_sem=in_sems.at[quarter, slot],
            device_id={"seq": target},
            device_id_type=MESH,
        )

    def ring(quarter, slot):
        owner, target = [
            (seat, right),
            (seat, left),
            (left, right) if 2 * quarter < quarters else (right, left),
        ][slot]
        return send(quarter, owner, target, ring_out, ring_in, slot)

    def pair(quarter, slot):
        return send(quarter, (seat, left, right, across)[slot], partner, pair_out, pair_in, slot)

    def arrive(quarter):
        @pl.loop(quarter * turns, min((quarter + 1) * turns, count - 1))
        def _(turn):
            row_copy(turn).wait_recv()

        if quarter == quarters - 1:
            own.wait()
        arrived = got[quarter * turns : (quarter + 1) * turns].astype(jnp.float32)
        arrived = arrived.reshape(rows, full.shape[3])
        full[quarter, seat, :, :depth] = norm_rows(arrived[:, :depth], gain[...]).astype(jnp.bfloat16)
        full[quarter, seat, :, depth:] = arrived[:, depth:].astype(jnp.bfloat16)
        ring(quarter, 0).start()
        ring(quarter, 1).start()
        pair(quarter, 0).start()

    def forward(quarter):
        ring(quarter, 0).wait_recv()
        if 2 * quarter < quarters:
            ring(quarter, 2).start()
        pair(quarter, 1).start()
        ring(quarter, 1).wait_recv()
        if 2 * quarter >= quarters:
            ring(quarter, 2).start()
        pair(quarter, 2).start()

    def finish(quarter):
        ring(quarter, 2).wait_recv()
        pair(quarter, 3).start()
        for slot in range(4):
            pair(quarter, slot).wait_recv()
        block = full[quarter, :, :, :depth].reshape(seats * rows, depth)
        part = half_silu(0.5 * jnp.dot(block, w_ref[...], preferred_element_type=jnp.float32))
        mixed[:, quarter] = part.astype(jnp.bfloat16).reshape(seats, rows, part.shape[1])

    for k in (1, 2, 3):
        to_chip(k).start()
    to_partner(0).start()
    for quarter in range(quarters):
        arrive(quarter)
        if quarter == 0:
            for k in (1, 3, 2):
                to_chip(k).wait_recv()
                to_partner(k).start()
        if quarter >= 1:
            forward(quarter - 1)
        if quarter >= 2:
            finish(quarter - 2)
    forward(quarters - 1)
    finish(quarters - 2)
    finish(quarters - 1)

    total = quarters * rows
    first = (lax.broadcasted_iota(jnp.int32, (8, 128), 1) == 0).astype(jnp.bfloat16)
    places = lax.broadcasted_iota(jnp.int32, (total, total), 0).astype(jnp.float32)

    @pl.loop(0, seats)
    def _(owner):
        tags = jnp.concatenate([full[quarter, owner, :, depth:] for quarter in range(quarters)], axis=0)
        tag_row = lax.dot_general(
            first, tags, (((1,), (1,)), ((), ())), preferred_element_type=jnp.float32
        )[0:1]
        chosen = (places == tag_row).astype(jnp.bfloat16)
        arrived = mixed[owner].reshape(total, mixed.shape[3])
        there = pl.ds(pl.multiple_of(owner * total, total), total)
        proj[there, :] = jnp.dot(chosen, arrived, preferred_element_type=jnp.float32).astype(
            jnp.bfloat16
        )

    tags = jnp.concatenate([full[quarter, seat, :, depth:] for quarter in range(quarters)], axis=0)
    tags = jnp.concatenate([tags.astype(jnp.float32)] * (total // 128), axis=1)
    columns = lax.broadcasted_iota(jnp.int32, (total, total), 1).astype(jnp.float32)
    to_place[...] = (tags == columns).astype(jnp.bfloat16)

    for k in (1, 2, 3):
        to_chip(k).wait_send()
    for k in range(4):
        to_partner(k).wait()
    for quarter in range(quarters):
        for slot in range(3):
            ring(quarter, slot).wait_send()
        for slot in range(4):
            pair(quarter, slot).wait_send()

    @pl.loop(0, count - 1)
    def _(turn):
        row_copy(turn).wait_send()

    own_w.wait()


def tail_kernel(
    longest, peers, table, proj, gain_ref, row_ids, col_ids, w_full, to_place, home,
    bias, acc, gated, mine, returned, swap_out, swap_in, back_out, back_in, own_sem,
):
    me = lax.axis_index("dp")
    seat = lax.axis_index("seq")
    seats = lax.axis_size("seq")
    reach = bias.shape[0]
    width = acc.shape[1]
    barrier = pltpu.get_barrier_semaphore()

    @pl.loop(1, peers)
    def _(distance):
        pl.semaphore_signal(
            barrier, inc=1, device_id={"dp": (me + distance) % peers}, device_id_type=MESH
        )

    reach_all(barrier, [{"seq": (seat + k) % seats} for k in range(1, seats)])

    for offset in range(reach):
        bias[offset] = half_bias(table, offset, longest, table.shape[1])
    scale = 0.5 * width ** (-0.5)

    def swap(distance):
        return pltpu.make_async_remote_copy(
            src_ref=gated.at[(seat + distance) % seats],
            dst_ref=mine.at[seat],
            send_sem=swap_out.at[distance],
            recv_sem=swap_in.at[distance],
            device_id={"seq": (seat + distance) % seats},
            device_id_type=MESH,
        )

    @pl.loop(1, seats + 1)
    def _(distance):
        block = (seat + distance) % seats
        here = pl.ds(pl.multiple_of(block * BLOCK, BLOCK), BLOCK)
        ids = jnp.concatenate([col_ids[here, :]] * (BLOCK // col_ids.shape[1]), axis=1)

        def term(offset):
            there = pl.ds(pl.multiple_of((block - offset) * BLOCK, BLOCK), BLOCK)
            scores = lax.dot_general(
                proj[here, :width],
                proj[there, width : 2 * width],
                (((1,), (1,)), ((), ())),
                preferred_element_type=jnp.float32,
            )
            weights = half_silu(scores * scale + bias[offset])
            weights = jnp.where(ids == row_ids[:, there], weights, 0.0).astype(jnp.bfloat16)
            return jnp.dot(
                weights, proj[there, 2 * width : 3 * width], preferred_element_type=jnp.float32
            )

        acc[...] = term(0)

        @pl.when(distance == 2)
        def _():
            pl.semaphore_wait(barrier, peers - 1 + seats - 1)

        @pl.when(distance >= 2)
        def _():
            swap(distance - 1).start()

        for offset in range(1, reach):

            @pl.when(block >= offset)
            def _(offset=offset):
                acc[...] += term(offset)

        gate = proj[here, 3 * width :].astype(jnp.float32)
        gated[block] = (norm_rows(acc[...], gain_ref[...]) * gate).astype(jnp.bfloat16)

    mine[seat] = gated[seat]
    for distance in range(1, seats):
        swap(distance).wait_recv()
    rows = jnp.concatenate([mine[head] for head in range(seats)], axis=1)
    merged = jnp.dot(rows, w_full[...], preferred_element_type=jnp.float32).astype(jnp.bfloat16)
    picked = jnp.dot(to_place[...], merged, preferred_element_type=jnp.float32)
    returned[...] = picked.reshape(returned.shape).astype(jnp.bfloat16)
    for distance in range(1, seats):
        swap(distance).wait_send()

    def back(turn):
        peer = (me + peers - far_first(turn, peers)) % peers
        return pltpu.make_async_remote_copy(
            src_ref=returned.at[turn],
            dst_ref=home.at[me],
            send_sem=back_out.at[turn],
            recv_sem=back_in.at[turn],
            device_id={"dp": peer},
            device_id_type=MESH,
        )

    @pl.loop(0, peers - 1)
    def _(turn):
        back(turn).start()

    own = pltpu.make_async_copy(returned.at[peers - 1], home.at[me], own_sem)
    own.start()

    @pl.loop(0, peers - 1)
    def _(turn):
        back(turn).wait()

    own.wait()


IN_VMEM = pl.BlockSpec(memory_space=pltpu.VMEM)
DMA = pltpu.SemaphoreType.DMA


def remote(kernel, number, operands, shapes, scratch):
    return pl.pallas_call(
        kernel,
        out_shape=tuple(jax.ShapeDtypeStruct(shape, jnp.bfloat16) for shape in shapes),
        in_specs=[IN_VMEM] * len(operands),
        out_specs=(IN_VMEM,) * len(shapes),
        scratch_shapes=scratch,
        compiler_params=pltpu.CompilerParams(
            collective_id=number, has_side_effects=True, vmem_limit_bytes=32 << 20
        ),
    )(*operands)


def enter(sent, shard, gain, w_project, quarters=4):
    count, seats = lax.axis_size("dp"), lax.axis_size("seq")
    peers, each, wide = sent.shape
    rows, width = peers * each // quarters, w_project.shape[1]
    return remote(
        functools.partial(enter_kernel, count, quarters),
        0,
        (sent, shard, gain[None], w_project),
        (
            (seats,) + shard.shape,
            (seats * quarters * rows, width),
            (quarters * rows, quarters * rows),
        ),
        [
            pltpu.VMEM(sent.shape, jnp.bfloat16),
            pltpu.VMEM((quarters, seats, rows, wide), jnp.bfloat16),
            pltpu.VMEM((seats, quarters, rows, width), jnp.bfloat16),
            DMA((count,)),
            DMA((count,)),
            DMA((8,)),
            DMA((8,)),
            DMA((quarters, 3)),
            DMA((quarters, 3)),
            DMA((quarters, 4)),
            DMA((quarters, 4)),
            DMA((2,)),
        ],
    )


def tail(proj, table, gain, segment, w_full, to_place):
    peers, seats = lax.axis_size("dp"), lax.axis_size("seq")
    count, (width,), depth = proj.shape[0], gain.shape, w_full.shape[1]
    rows = to_place.shape[0]
    reach = count // 2 // BLOCK + 1
    return pl.pallas_call(
        functools.partial(tail_kernel, count // 2, peers),
        out_shape=jax.ShapeDtypeStruct((peers, rows // peers, depth), jnp.bfloat16),
        in_specs=[pl.BlockSpec(memory_space=pltpu.SMEM)] + [IN_VMEM] * 6,
        out_specs=IN_VMEM,
        scratch_shapes=[
            pltpu.VMEM((reach, BLOCK, BLOCK), jnp.float32),
            pltpu.VMEM((BLOCK, width), jnp.float32),
            pltpu.VMEM((seats, rows, width), jnp.bfloat16),
            pltpu.VMEM((seats, rows, width), jnp.bfloat16),
            pltpu.VMEM((peers, rows // peers, depth), jnp.bfloat16),
            DMA((seats,)),
            DMA((seats,)),
            DMA((peers,)),
            DMA((peers,)),
            DMA(()),
        ],
        compiler_params=pltpu.CompilerParams(
            collective_id=2, has_side_effects=True, vmem_limit_bytes=32 << 20
        ),
    )(
        table,
        proj,
        gain[None],
        segment,
        jnp.broadcast_to(segment.reshape(count, 1), (count, 128)),
        w_full,
        to_place,
    )


def pick(chosen, rows, dim):
    return lax.dot_general(
        chosen, rows, (((dim,), (0,)), ((), ())), preferred_element_type=jnp.float32
    ).astype(jnp.bfloat16)


def local(events, w_project, w_output, rel_bias, in_gain, out_gain, user_ids, owner_dev, owner_row):
    peers = lax.axis_size("dp")
    count, depth = events.shape[1:]
    each = count // peers
    owners = owner_dev[0]
    index = jnp.arange(count, dtype=jnp.int32)
    earlier = (owners[:, None] == owners[None, :]) & (index[None, :] < index[:, None])
    slot = owners * each + jnp.sum(earlier.astype(jnp.int32), axis=1)
    to_slot = (slot[None, :] == index[:, None]).astype(jnp.bfloat16)
    tagged = jnp.concatenate(
        [events[0], jnp.broadcast_to(owner_row[0][:, None], (count, 128)).astype(jnp.bfloat16)], axis=1
    )
    sent = pick(to_slot, tagged, 1)
    w_full, proj, to_place = enter(
        sent.reshape(peers, each, depth + 128), w_output, in_gain, w_project
    )
    home = tail(proj, rel_bias, out_gain, user_ids, w_full.reshape(-1, depth), to_place)
    home = home.reshape(count, depth)
    return pick(to_slot, home, 0)[None]


def solution(mesh):
    return jax.shard_map(
        local,
        mesh=mesh,
        in_specs=(
            P("dp", "seq", None),
            P(None, "seq"),
            P("seq", None),
            P("seq", None),
            P(),
            P("seq"),
            P("dp", None),
            P("dp", "seq"),
            P("dp", "seq"),
        ),
        out_specs=P("dp", "seq", None),
        check_vma=False,
    )
```

```python
import functools

import jax
import jax.numpy as jnp
from jax import lax
from jax.experimental import pallas as pl
from jax.experimental.pallas import tpu as pltpu
from jax.sharding import PartitionSpec as P

EPSILON = 1e-05
BLOCK = 256
FAR = -1e30
MESH = pl.DeviceIdType.MESH


def norm_rows(values, gain):
    average = jnp.mean(values, axis=-1, keepdims=True)
    centred = values - average
    spread = jnp.mean(centred * centred, axis=-1, keepdims=True)
    return centred * lax.rsqrt(spread + EPSILON) * gain


def half_silu(half):
    return half + half * jnp.tanh(half)


def half_bias(table, offset, longest, levels):
    rows = lax.broadcasted_iota(jnp.int32, (BLOCK, BLOCK), 0)
    columns = lax.broadcasted_iota(jnp.int32, (BLOCK, BLOCK), 1)
    distance = rows - columns + offset * BLOCK
    total = jnp.full((BLOCK, BLOCK), table[0, 0], jnp.float32)
    for level in range(levels - 1):
        threshold = longest // 2 ** (levels - 1 - level)
        step = table[0, level + 1] - table[0, level]
        if threshold > offset * BLOCK + BLOCK - 1:
            continue
        if threshold <= offset * BLOCK - BLOCK + 1:
            total = total + step
        else:
            total = total + jnp.where(distance >= threshold, step, 0.0)
    total = 0.5 * total
    if offset == 0:
        total = jnp.where(distance >= 0, total, FAR)
    return total


def reach_all(barrier, places):
    for place in places:
        pl.semaphore_signal(barrier, inc=1, device_id=place, device_id_type=MESH)


def near_first(turn, count):
    mirrored = count - 2 - turn
    return count // 2 - (mirrored + 1) // 2 * (2 * (mirrored % 2) - 1)


def enter_kernel(
    count, quarters, sent, shard, gain, w_ref, full_w, proj, to_place,
    got, full, mixed, out_sem, in_sem, w_out, w_in, ring_out, ring_in, pair_out, pair_in, own_sem,
):
    me = lax.axis_index("dp")
    seat = lax.axis_index("seq")
    seats = lax.axis_size("seq")
    partner = seat + 1 - 2 * (seat % 2)
    right, left, across = (seat + 2) % seats, (seat + seats - 2) % seats, (seat + 4) % seats
    turns = count // quarters
    rows = full.shape[2]
    depth = gain.shape[1]
    barrier = pltpu.get_barrier_semaphore()

    @pl.loop(1, count)
    def _(distance):
        pl.semaphore_signal(
            barrier, inc=1, device_id={"dp": (me + distance) % count}, device_id_type=MESH
        )

    reach_all(barrier, [{"seq": place} for place in (partner, right, left, across)])
    pl.semaphore_wait(barrier, count - 1 + 4)

    def row_copy(turn):
        peer = (me + near_first(turn, count)) % count
        return pltpu.make_async_remote_copy(
            src_ref=sent.at[peer],
            dst_ref=got.at[turn],
            send_sem=out_sem.at[turn],
            recv_sem=in_sem.at[turn],
            device_id={"dp": peer},
            device_id_type=MESH,
        )

    @pl.loop(0, count - 1)
    def _(turn):
        row_copy(turn).start()

    own = pltpu.make_async_copy(sent.at[me], got.at[count - 1], own_sem.at[0])
    own.start()
    own_w = pltpu.make_async_copy(shard, full_w.at[seat], own_sem.at[1])
    own_w.start()

    def to_chip(k):
        return pltpu.make_async_remote_copy(
            src_ref=shard,
            dst_ref=full_w.at[seat],
            send_sem=w_out.at[k],
            recv_sem=w_in.at[k],
            device_id={"seq": (seat + 2 * k) % seats},
            device_id_type=MESH,
        )

    def to_partner(k):
        block = full_w.at[(seat + seats - 2 * k) % seats]
        return pltpu.make_async_remote_copy(
            src_ref=shard if k == 0 else block,
            dst_ref=block,
            send_sem=w_out.at[4 + k],
            recv_sem=w_in.at[4 + k],
            device_id={"seq": partner},
            device_id_type=MESH,
        )

    def send(quarter, owner, target, out_sems, in_sems, slot):
        block = full.at[quarter, owner]
        return pltpu.make_async_remote_copy(
            src_ref=block,
            dst_ref=block,
            send_sem=out_sems.at[quarter, slot],
            recv_sem=in_sems.at[quarter, slot],
            device_id={"seq": target},
            device_id_type=MESH,
        )

    def ring(quarter, slot):
        owner, target = [
            (seat, right),
            (seat, left),
            (left, right) if 2 * quarter < quarters else (right, left),
        ][slot]
        return send(quarter, owner, target, ring_out, ring_in, slot)

    def pair(quarter, slot):
        return send(quarter, (seat, left, right, across)[slot], partner, pair_out, pair_in, slot)

    def arrive(quarter):
        @pl.loop(quarter * turns, min((quarter + 1) * turns, count - 1))
        def _(turn):
            row_copy(turn).wait_recv()

        if quarter == quarters - 1:
            own.wait()
        arrived = got[quarter * turns : (quarter + 1) * turns].astype(jnp.float32)
        arrived = arrived.reshape(rows, full.shape[3])
        full[quarter, seat, :, :depth] = norm_rows(arrived[:, :depth], gain[...]).astype(jnp.bfloat16)
        full[quarter, seat, :, depth:] = arrived[:, depth:].astype(jnp.bfloat16)
        ring(quarter, 0).start()
        ring(quarter, 1).start()
        pair(quarter, 0).start()

    def forward(quarter):
        ring(quarter, 0).wait_recv()
        if 2 * quarter < quarters:
            ring(quarter, 2).start()
        pair(quarter, 1).start()
        ring(quarter, 1).wait_recv()
        if 2 * quarter >= quarters:
            ring(quarter, 2).start()
        pair(quarter, 2).start()

    def finish(quarter):
        ring(quarter, 2).wait_recv()
        pair(quarter, 3).start()
        for slot in range(4):
            pair(quarter, slot).wait_recv()
        block = full[quarter, :, :, :depth].reshape(seats * rows, depth)
        part = half_silu(0.5 * jnp.dot(block, w_ref[...], preferred_element_type=jnp.float32))
        mixed[:, quarter] = part.astype(jnp.bfloat16).reshape(seats, rows, part.shape[1])

    for k in (1, 2, 3):
        to_chip(k).start()
    to_partner(0).start()
    for quarter in range(quarters):
        arrive(quarter)
        if quarter == 0:
            for k in (1, 3, 2):
                to_chip(k).wait_recv()
                to_partner(k).start()
        if quarter >= 1:
            forward(quarter - 1)
        if quarter >= 2:
            finish(quarter - 2)
    forward(quarters - 1)
    finish(quarters - 2)
    finish(quarters - 1)

    total = quarters * rows
    first = (lax.broadcasted_iota(jnp.int32, (8, 128), 1) == 0).astype(jnp.bfloat16)
    places = lax.broadcasted_iota(jnp.int32, (total, total), 0).astype(jnp.float32)

    @pl.loop(0, seats)
    def _(owner):
        tags = jnp.concatenate([full[quarter, owner, :, depth:] for quarter in range(quarters)], axis=0)
        tag_row = lax.dot_general(
            first, tags, (((1,), (1,)), ((), ())), preferred_element_type=jnp.float32
        )[0:1]
        chosen = (places == tag_row).astype(jnp.bfloat16)
        arrived = mixed[owner].reshape(total, mixed.shape[3])
        there = pl.ds(pl.multiple_of(owner * total, total), total)
        proj[there, :] = jnp.dot(chosen, arrived, preferred_element_type=jnp.float32).astype(
            jnp.bfloat16
        )

    tags = jnp.concatenate([full[quarter, seat, :, depth:] for quarter in range(quarters)], axis=0)
    tags = jnp.concatenate([tags.astype(jnp.float32)] * (total // 128), axis=1)
    columns = lax.broadcasted_iota(jnp.int32, (total, total), 1).astype(jnp.float32)
    to_place[...] = (tags == columns).astype(jnp.bfloat16)

    for k in (1, 2, 3):
        to_chip(k).wait_send()
    for k in range(4):
        to_partner(k).wait()
    for quarter in range(quarters):
        for slot in range(3):
            ring(quarter, slot).wait_send()
        for slot in range(4):
            pair(quarter, slot).wait_send()

    @pl.loop(0, count - 1)
    def _(turn):
        row_copy(turn).wait_send()

    own_w.wait()


def tail_kernel(
    longest, peers, table, proj, gain_ref, row_ids, col_ids, w_full, to_place, home,
    bias, acc, gated, mine, returned, swap_out, swap_in, back_out, back_in, own_sem,
):
    me = lax.axis_index("dp")
    seat = lax.axis_index("seq")
    seats = lax.axis_size("seq")
    reach = bias.shape[0]
    width = acc.shape[1]
    barrier = pltpu.get_barrier_semaphore()

    @pl.loop(1, peers)
    def _(distance):
        pl.semaphore_signal(
            barrier, inc=1, device_id={"dp": (me + distance) % peers}, device_id_type=MESH
        )

    reach_all(barrier, [{"seq": (seat + k) % seats} for k in range(1, seats)])

    for offset in range(reach):
        bias[offset] = half_bias(table, offset, longest, table.shape[1])
    scale = 0.5 * width ** (-0.5)

    def swap(distance):
        return pltpu.make_async_remote_copy(
            src_ref=gated.at[(seat + distance) % seats],
            dst_ref=mine.at[seat],
            send_sem=swap_out.at[distance],
            recv_sem=swap_in.at[distance],
            device_id={"seq": (seat + distance) % seats},
            device_id_type=MESH,
        )

    @pl.loop(1, seats + 1)
    def _(distance):
        block = (seat + distance) % seats
        here = pl.ds(pl.multiple_of(block * BLOCK, BLOCK), BLOCK)
        ids = jnp.concatenate([col_ids[here, :]] * (BLOCK // col_ids.shape[1]), axis=1)

        def term(offset):
            there = pl.ds(pl.multiple_of((block - offset) * BLOCK, BLOCK), BLOCK)
            scores = lax.dot_general(
                proj[here, :width],
                proj[there, width : 2 * width],
                (((1,), (1,)), ((), ())),
                preferred_element_type=jnp.float32,
            )
            weights = half_silu(scores * scale + bias[offset])
            weights = jnp.where(ids == row_ids[:, there], weights, 0.0).astype(jnp.bfloat16)
            return jnp.dot(
                weights, proj[there, 2 * width : 3 * width], preferred_element_type=jnp.float32
            )

        acc[...] = term(0)

        @pl.when(distance == 2)
        def _():
            pl.semaphore_wait(barrier, peers - 1 + seats - 1)

        @pl.when(distance >= 2)
        def _():
            swap(distance - 1).start()

        for offset in range(1, reach):

            @pl.when(block >= offset)
            def _(offset=offset):
                acc[...] += term(offset)

        gate = proj[here, 3 * width :].astype(jnp.float32)
        gated[block] = (norm_rows(acc[...], gain_ref[...]) * gate).astype(jnp.bfloat16)

    mine[seat] = gated[seat]
    for distance in range(1, seats):
        swap(distance).wait_recv()
    rows = jnp.concatenate([mine[head] for head in range(seats)], axis=1)
    merged = jnp.dot(rows, w_full[...], preferred_element_type=jnp.float32).astype(jnp.bfloat16)
    picked = jnp.dot(to_place[...], merged, preferred_element_type=jnp.float32)
    returned[...] = picked.reshape(returned.shape).astype(jnp.bfloat16)
    for distance in range(1, seats):
        swap(distance).wait_send()

    def back(turn):
        peer = (me + peers - near_first(turn, peers)) % peers
        return pltpu.make_async_remote_copy(
            src_ref=returned.at[turn],
            dst_ref=home.at[me],
            send_sem=back_out.at[turn],
            recv_sem=back_in.at[turn],
            device_id={"dp": peer},
            device_id_type=MESH,
        )

    @pl.loop(0, peers - 1)
    def _(turn):
        back(peers - 2 - turn).start()

    own = pltpu.make_async_copy(returned.at[peers - 1], home.at[me], own_sem)
    own.start()

    @pl.loop(0, peers - 1)
    def _(turn):
        back(turn).wait()

    own.wait()


IN_VMEM = pl.BlockSpec(memory_space=pltpu.VMEM)
DMA = pltpu.SemaphoreType.DMA


def remote(kernel, number, operands, shapes, scratch):
    return pl.pallas_call(
        kernel,
        out_shape=tuple(jax.ShapeDtypeStruct(shape, jnp.bfloat16) for shape in shapes),
        in_specs=[IN_VMEM] * len(operands),
        out_specs=(IN_VMEM,) * len(shapes),
        scratch_shapes=scratch,
        compiler_params=pltpu.CompilerParams(
            collective_id=number, has_side_effects=True, vmem_limit_bytes=32 << 20
        ),
    )(*operands)


def enter(sent, shard, gain, w_project, quarters=4):
    count, seats = lax.axis_size("dp"), lax.axis_size("seq")
    peers, each, wide = sent.shape
    rows, width = peers * each // quarters, w_project.shape[1]
    return remote(
        functools.partial(enter_kernel, count, quarters),
        0,
        (sent, shard, gain[None], w_project),
        (
            (seats,) + shard.shape,
            (seats * quarters * rows, width),
            (quarters * rows, quarters * rows),
        ),
        [
            pltpu.VMEM(sent.shape, jnp.bfloat16),
            pltpu.VMEM((quarters, seats, rows, wide), jnp.bfloat16),
            pltpu.VMEM((seats, quarters, rows, width), jnp.bfloat16),
            DMA((count,)),
            DMA((count,)),
            DMA((8,)),
            DMA((8,)),
            DMA((quarters, 3)),
            DMA((quarters, 3)),
            DMA((quarters, 4)),
            DMA((quarters, 4)),
            DMA((2,)),
        ],
    )


def tail(proj, table, gain, segment, w_full, to_place):
    peers, seats = lax.axis_size("dp"), lax.axis_size("seq")
    count, (width,), depth = proj.shape[0], gain.shape, w_full.shape[1]
    rows = to_place.shape[0]
    reach = count // 2 // BLOCK + 1
    return pl.pallas_call(
        functools.partial(tail_kernel, count // 2, peers),
        out_shape=jax.ShapeDtypeStruct((peers, rows // peers, depth), jnp.bfloat16),
        in_specs=[pl.BlockSpec(memory_space=pltpu.SMEM)] + [IN_VMEM] * 6,
        out_specs=IN_VMEM,
        scratch_shapes=[
            pltpu.VMEM((reach, BLOCK, BLOCK), jnp.float32),
            pltpu.VMEM((BLOCK, width), jnp.float32),
            pltpu.VMEM((seats, rows, width), jnp.bfloat16),
            pltpu.VMEM((seats, rows, width), jnp.bfloat16),
            pltpu.VMEM((peers, rows // peers, depth), jnp.bfloat16),
            DMA((seats,)),
            DMA((seats,)),
            DMA((peers,)),
            DMA((peers,)),
            DMA(()),
        ],
        compiler_params=pltpu.CompilerParams(
            collective_id=2, has_side_effects=True, vmem_limit_bytes=32 << 20
        ),
    )(
        table,
        proj,
        gain[None],
        segment,
        jnp.broadcast_to(segment.reshape(count, 1), (count, 128)),
        w_full,
        to_place,
    )


def pick(chosen, rows, dim):
    return lax.dot_general(
        chosen, rows, (((dim,), (0,)), ((), ())), preferred_element_type=jnp.float32
    ).astype(jnp.bfloat16)


def local(events, w_project, w_output, rel_bias, in_gain, out_gain, user_ids, owner_dev, owner_row):
    peers = lax.axis_size("dp")
    count, depth = events.shape[1:]
    each = count // peers
    owners = owner_dev[0]
    index = jnp.arange(count, dtype=jnp.int32)
    earlier = (owners[:, None] == owners[None, :]) & (index[None, :] < index[:, None])
    slot = owners * each + jnp.sum(earlier.astype(jnp.int32), axis=1)
    to_slot = (slot[None, :] == index[:, None]).astype(jnp.bfloat16)
    tagged = jnp.concatenate(
        [events[0], jnp.broadcast_to(owner_row[0][:, None], (count, 128)).astype(jnp.bfloat16)], axis=1
    )
    sent = pick(to_slot, tagged, 1)
    w_full, proj, to_place = enter(
        sent.reshape(peers, each, depth + 128), w_output, in_gain, w_project
    )
    home = tail(proj, rel_bias, out_gain, user_ids, w_full.reshape(-1, depth), to_place)
    home = home.reshape(count, depth)
    return pick(to_slot, home, 0)[None]


def solution(mesh):
    return jax.shard_map(
        local,
        mesh=mesh,
        in_specs=(
            P("dp", "seq", None),
            P(None, "seq"),
            P("seq", None),
            P("seq", None),
            P(),
            P("seq"),
            P("dp", None),
            P("dp", "seq"),
            P("dp", "seq"),
        ),
        out_specs=P("dp", "seq", None),
        check_vma=False,
    )
```
